32 devices in a mesh: dp: 4 (over z), seq: 4 (over y, x), tensor: 2 (over core).
Axes of the slice: x: 2, y: 2, z: 4, core: 2. Of those that a mesh axis runs over, the one named last changes fastest.
Arguments:
- hidden_in: float32 [2048, 1024], P(('dp', 'seq')), may hold values from -6 to 6
- cotangent: float32 [2048, 1024], P(('dp', 'seq')), may hold values from -6 to 6
- segment_ids: int32 [2048], P('dp'), may hold values from 0 to 3, as said below
- positions: int32 [2048], P('dp'), may hold values from 0 to 511, as said below
- w_query: bfloat16 [1024, 1024], P('dp', 'tensor'), may hold values from -0.1875 to 0.1875
- w_key: bfloat16 [1024, 256], P('dp', 'tensor'), may hold values from -0.1875 to 0.1875
- w_value: bfloat16 [1024, 256], P('dp', 'tensor'), may hold values from -0.1875 to 0.1875
- w_mamba_gate: bfloat16 [1024, 1536], P('dp', 'tensor'), may hold values from -0.1875 to 0.1875
- w_mamba_in: bfloat16 [1024, 1536], P('dp', 'tensor'), may hold values from -0.1875 to 0.1875
- w_mamba_bcdt: bfloat16 [1024, 280], P('dp'), may hold values from -0.1875 to 0.1875
- w_attention_out: bfloat16 [1024, 1024], P('tensor', 'dp'), may hold values from -0.5 to 0.5
- w_mamba_out: bfloat16 [1536, 1024], P('tensor', 'dp'), may hold values from -0.15625 to 0.15625
- w_feed_gate: bfloat16 [1024, 2048], P('dp', 'tensor'), may hold values from -0.1875 to 0.1875
- w_feed_up: bfloat16 [1024, 2048], P('dp', 'tensor'), may hold values from -0.1875 to 0.1875
- w_feed_down: bfloat16 [2048, 1024], P('tensor', 'dp'), may hold values from -0.125 to 0.125
- gain_mixer: bfloat16 [1024], P('dp'), may hold values from 0.5 to 1.5
- gain_feed: bfloat16 [1024], P('dp'), may hold values from 0.5 to 1.5
- conv_weight: float32 [4, 1792], replicated, may hold values from -0.6 to 0.6
- log_decay: float32 [24], replicated, may hold values from -3 to 0.7
- step_bias: float32 [24], replicated, may hold values from -5 to -3
- skip_scale: float32 [24], replicated, may hold values from 0.5 to 1.5
Outputs:
- output: float32 [2048, 1024], P(('dp', 'seq'))
- grad_hidden: float32 [2048, 1024], P(('dp', 'seq'))
- grad_w_query: float32 [1024, 1024], P('dp', 'tensor')
- grad_w_key: float32 [1024, 256], P('dp', 'tensor')
- grad_w_value: float32 [1024, 256], P('dp', 'tensor')
- grad_w_mamba_gate: float32 [1024, 1536], P('dp', 'tensor')
- grad_w_mamba_in: float32 [1024, 1536], P('dp', 'tensor')
- grad_w_mamba_bcdt: float32 [1024, 280], P('dp')
- grad_w_attention_out: float32 [1024, 1024], P('tensor', 'dp')
- grad_w_mamba_out: float32 [1536, 1024], P('tensor', 'dp')
- grad_w_feed_gate: float32 [1024, 2048], P('dp', 'tensor')
- grad_w_feed_up: float32 [1024, 2048], P('dp', 'tensor')
- grad_w_feed_down: float32 [2048, 1024], P('tensor', 'dp')
- grad_gain_mixer: float32 [1024], P('dp')
- grad_gain_feed: float32 [1024], P('dp')
- grad_conv_weight: float32 [4, 1792], replicated
- grad_log_decay: float32 [24], replicated
- grad_step_bias: float32 [24], replicated
- grad_skip_scale: float32 [24], replicated
The draws below stay inside these ranges and needn't reach their ends.
Inputs may be any that keep to these rules, and one draw needn't show every extreme that they name: `segment_ids`: within each aligned block of 512 tokens the ids number its sequences 0, 1, 2 ... in order; each sequence covers whole consecutive blocks of 128 tokens; the first run holds one sequence, the last run one sequence a block. `positions`: the index of each token within its sequence, counted from 0.
All inputs are finite; a program needn't handle non-finite values.
Results may differ from the reference program's by a relative error of at most 0.015.
Values may be sent and summed in bfloat16 or wider, within the bound.
A program may use at most 128 MiB of HBM per device.

```python
import functools
import math
import jax
import jax.numpy as jnp
from jax import lax

D = 1024
QH = 8
KVH = 2
HD = 128
MH = 24
MP = 64
NS = 128
KCONV = 4
FF = 2048
BLOCK = 128
MD = 1536
QCOL = 1024
KVCOL = 256
BCD = 280
CONVW = 1792
GROUP = 512
TOKENS = 2048
N_SEQ = 4
N_TENSOR = 2


def block_layout(key):
    base_key = jax.random.fold_in(key, 31)
    odds_key, cut_key = jax.random.split(base_key)
    group_count = TOKENS // GROUP
    block_count = GROUP // BLOCK
    cut_odds = jax.random.randint(odds_key, (group_count, 1), 0, 4)
    cut_draws = jax.random.randint(cut_key, (group_count, block_count), 0, 4)
    cut_flags = (cut_draws < cut_odds).astype(jnp.int32)
    group_index = jnp.arange(group_count, dtype=jnp.int32)[:, None]
    block_index = jnp.arange(block_count, dtype=jnp.int32)[None, :]
    cut_flags = jnp.where(group_index == group_count - 1, 1, cut_flags)
    cut_flags = jnp.where(group_index == 0, 0, cut_flags)
    cut_flags = jnp.where(block_index == 0, 1, cut_flags)
    sequence = jnp.cumsum(cut_flags, axis=1) - 1
    seq_start = lax.cummax(jnp.where(cut_flags == 1, block_index, 0), axis=1)
    offset = jnp.arange(BLOCK, dtype=jnp.int32)
    token_seq = jnp.repeat(sequence, BLOCK, axis=1).reshape(TOKENS)
    token_pos = ((block_index - seq_start)[:, :, None] * BLOCK + offset[None, None, :]).reshape(TOKENS)
    return (token_seq.astype(jnp.int32), token_pos.astype(jnp.int32))


def draw_segment_ids(key, part):
    return block_layout(key)[0]


def draw_positions(key, part):
    return block_layout(key)[1]


def steps_of(key, shape, cuts, low, largest):
    level, own = 1.0, jax.random.fold_in(key, 6)
    for axis_at, blocks in cuts:
        draws = jnp.exp(jax.random.uniform(jax.random.fold_in(own, axis_at), (blocks,), jnp.float32, low / len(cuts), largest / len(cuts)))
        level = level * jnp.repeat(draws, shape[axis_at] // blocks).reshape([-1 if axis == axis_at else 1 for axis in range(len(shape))])
    return level


def normal_values(stream_key, dims, spread, bound, pieces=(), kind=jnp.bfloat16):
    array = spread * jax.random.normal(stream_key, dims, jnp.float32)
    if pieces:
        array = array * steps_of(stream_key, dims, pieces, -0.22, 0.18)
    return jnp.clip(array, -bound, bound).astype(kind)


def setup_inputs(seed: int = 0) -> dict:
    splits = jax.random.split(jax.random.key(seed), 22)
    hidden_in = normal_values(splits[0], (TOKENS, D), 1.0, 6.0, ((0, 16),), jnp.float32)
    cotangent = normal_values(splits[1], (TOKENS, D), 1.0, 6.0, ((0, 16),), jnp.float32)
    segment_ids = draw_segment_ids(jax.random.fold_in(splits[21], 71), 0)
    positions = draw_positions(jax.random.fold_in(splits[21], 71), 0)
    w_query = normal_values(splits[4], (D, QCOL), D ** -0.5, 0.1875, ((0, 4), (1, 2)))
    w_key = normal_values(splits[5], (D, KVCOL), D ** -0.5, 0.1875, ((0, 4), (1, 2)))
    w_value = normal_values(splits[6], (D, KVCOL), D ** -0.5, 0.1875, ((0, 4), (1, 2)))
    w_mamba_gate = normal_values(splits[7], (D, MD), D ** -0.5, 0.1875, ((0, 4), (1, 2)))
    w_mamba_in = normal_values(splits[8], (D, MD), D ** -0.5, 0.1875, ((0, 4), (1, 2)))
    w_mamba_bcdt = normal_values(splits[9], (D, BCD), D ** -0.5, 0.1875, ((0, 4),))
    w_attention_out = normal_values(splits[10], (QCOL, D), HD ** -0.5, 0.5, ((0, 2), (1, 4)))
    w_mamba_out = normal_values(splits[11], (MD, D), MD ** -0.5, 0.15625, ((0, 2), (1, 4)))
    w_feed_gate = normal_values(splits[12], (D, FF), D ** -0.5, 0.1875, ((0, 4), (1, 2)))
    w_feed_up = normal_values(splits[13], (D, FF), D ** -0.5, 0.1875, ((0, 4), (1, 2)))
    w_feed_down = normal_values(splits[14], (FF, D), FF ** -0.5, 0.125, ((0, 2), (1, 4)))
    gain_mixer = jnp.clip(1.0 + 0.1 * jax.random.normal(splits[15], (D,), jnp.float32), 0.5, 1.5).astype(jnp.bfloat16)
    gain_feed = jnp.clip(1.0 + 0.1 * jax.random.normal(splits[16], (D,), jnp.float32), 0.5, 1.5).astype(jnp.bfloat16)
    conv_weight = jnp.clip(jax.random.uniform(splits[17], (KCONV, CONVW), jnp.float32, -0.6, 0.6), -0.6, 0.6)
    log_decay = jnp.clip(jax.random.uniform(splits[18], (MH,), jnp.float32, -3.0, 0.7), -3.0, 0.7)
    step_bias = jnp.clip(jax.random.uniform(splits[19], (MH,), jnp.float32, -5.0, -3.0), -5.0, -3.0)
    skip_scale = jnp.clip(jax.random.uniform(splits[20], (MH,), jnp.float32, 0.5, 1.5), 0.5, 1.5)
    return dict(hidden_in=hidden_in, cotangent=cotangent, segment_ids=segment_ids, positions=positions, w_query=w_query, w_key=w_key, w_value=w_value, w_mamba_gate=w_mamba_gate, w_mamba_in=w_mamba_in, w_mamba_bcdt=w_mamba_bcdt, w_attention_out=w_attention_out, w_mamba_out=w_mamba_out, w_feed_gate=w_feed_gate, w_feed_up=w_feed_up, w_feed_down=w_feed_down, gain_mixer=gain_mixer, gain_feed=gain_feed, conv_weight=conv_weight, log_decay=log_decay, step_bias=step_bias, skip_scale=skip_scale)


epsilon = 1e-05
rope_base = 100000000000.0
masked_score = -1e+30
highest = lax.Precision.HIGHEST

def matmul(left_in, right_in):
    return jnp.dot(left_in, right_in, preferred_element_type=jnp.float32)

def outer_product(left_in, right_in):
    return jnp.einsum('tc,td->cd', left_in, right_in, preferred_element_type=jnp.float32)

def back_product(grad_in, weight_in):
    return jnp.einsum('tc,dc->td', grad_in, weight_in, preferred_element_type=jnp.float32)

def rope_angles(token_pos, head_width):
    half_width = head_width // 2
    freq_index = jnp.arange(half_width, dtype=jnp.float32)
    inverse_freq = jnp.exp(freq_index * (-2.0 * math.log(rope_base) / head_width))
    angles = token_pos.astype(jnp.float32)[:, None] * inverse_freq[None, :]
    return (jnp.cos(angles), jnp.sin(angles))

def rotate(values, cosine, sine_vals):
    half_width = values.shape[-1] // 2
    first_half = values[..., :half_width]
    second_half = values[..., half_width:]
    cos_rows = cosine[:, None, :]
    sin_rows = sine_vals[:, None, :]
    return jnp.concatenate([first_half * cos_rows - second_half * sin_rows, second_half * cos_rows + first_half * sin_rows], axis=-1)

def rms_forward(values, gain_vec):
    scale_rows = lax.rsqrt(lax.optimization_barrier(jnp.mean(values * values, axis=1, keepdims=True)) + epsilon)
    normed = values * scale_rows
    return (normed, scale_rows, (normed * gain_vec.astype(jnp.float32)[None, :]).astype(jnp.bfloat16))

def rms_backward(grad_out, normed, scale_rows, gain_vec, upstream):
    grad_gain = lax.optimization_barrier(jnp.sum(grad_out * normed, axis=0))
    grad_normed = grad_out * gain_vec.astype(jnp.float32)[None, :]
    grad_in = upstream + scale_rows * (grad_normed - normed * lax.optimization_barrier(jnp.mean(grad_normed * normed, axis=1, keepdims=True)))
    return (grad_in, grad_gain)

def silu_slope(pre_act):
    sigmoid_gate = jax.nn.sigmoid(pre_act)
    return sigmoid_gate * (1.0 + pre_act * (1.0 - sigmoid_gate))

def attend_forward(query_in, key_in, value_in, allowed, score_scale):
    total_rows = query_in.shape[0]
    block_rows = min(total_rows, 512)
    block_count = total_rows // block_rows

    def one_block(block_index):
        row_start = block_index * block_rows
        query_rows = lax.dynamic_slice_in_dim(query_in, row_start, block_rows, 0)
        visible = lax.dynamic_slice_in_dim(allowed, row_start, block_rows, 0)
        scores = jnp.einsum('qd,kd->qk', query_rows, key_in, preferred_element_type=jnp.float32) * score_scale
        scores = jnp.where(visible, scores, masked_score)
        row_peak = lax.optimization_barrier(jnp.max(scores, axis=1, keepdims=True))
        logsum = row_peak + jnp.log(lax.optimization_barrier(jnp.sum(jnp.exp(scores - row_peak), axis=1, keepdims=True)))
        softmax_low = jnp.exp(scores - logsum).astype(jnp.bfloat16)
        result = jnp.dot(softmax_low, value_in, preferred_element_type=jnp.float32).astype(jnp.bfloat16)
        return (result, logsum[:, 0])
    result, logsum = lax.map(one_block, jnp.arange(block_count, dtype=jnp.int32))
    return (result.reshape(total_rows, value_in.shape[1]), logsum.reshape(total_rows))

def attend_backward(query_in, key_in, value_in, allowed, score_scale, result, logsum, grad_result):
    total_rows, head_width = query_in.shape
    block_rows = min(total_rows, 512)
    block_count = total_rows // block_rows
    row_delta = lax.optimization_barrier(jnp.sum(grad_result.astype(jnp.float32) * result.astype(jnp.float32), axis=1))

    def one_block(totals, block_index):
        grad_key, grad_value = totals
        row_start = block_index * block_rows
        query_rows = lax.dynamic_slice_in_dim(query_in, row_start, block_rows, 0)
        visible = lax.dynamic_slice_in_dim(allowed, row_start, block_rows, 0)
        grad_rows = lax.dynamic_slice_in_dim(grad_result, row_start, block_rows, 0)
        logsum_rows = lax.dynamic_slice_in_dim(logsum, row_start, block_rows, 0)
        delta_rows = lax.dynamic_slice_in_dim(row_delta, row_start, block_rows, 0)
        scores = jnp.einsum('qd,kd->qk', query_rows, key_in, preferred_element_type=jnp.float32) * score_scale
        scores = jnp.where(visible, scores, masked_score)
        softmax_f = jnp.exp(scores - logsum_rows[:, None])
        grad_value = grad_value + jnp.einsum('qk,qd->kd', softmax_f.astype(jnp.bfloat16), grad_rows, preferred_element_type=jnp.float32)
        grad_probs = jnp.einsum('qd,kd->qk', grad_rows, value_in, preferred_element_type=jnp.float32)
        grad_scores = (softmax_f * (grad_probs - delta_rows[:, None])).astype(jnp.bfloat16)
        grad_query = jnp.dot(grad_scores, key_in, preferred_element_type=jnp.float32) * score_scale
        grad_key = grad_key + jnp.einsum('qk,qd->kd', grad_scores, query_rows, preferred_element_type=jnp.float32) * score_scale
        return ((grad_key, grad_value), grad_query)
    zero_rows = jnp.zeros((total_rows, head_width), jnp.float32)
    (grad_key, grad_value), grad_query = lax.scan(one_block, (zero_rows, zero_rows), jnp.arange(block_count, dtype=jnp.int32))
    return (grad_query.reshape(total_rows, head_width), grad_key, grad_value)

def mamba_core(mixed_in, step_raw, conv_taps, log_rate, bias_step, skip_gain, segment_ids, allowed):
    total_rows, col_width = mixed_in.shape
    head_count = step_raw.shape[1]
    conv_sum = conv_taps[0][None, :] * mixed_in
    for shift_lag in range(1, conv_taps.shape[0]):
        shifted = jnp.concatenate([jnp.zeros((shift_lag, col_width), mixed_in.dtype), mixed_in[:-shift_lag]], axis=0)
        same_seq = jnp.concatenate([jnp.zeros((shift_lag,), dtype=bool), segment_ids[shift_lag:] == segment_ids[:-shift_lag]], axis=0)
        conv_sum = conv_sum + conv_taps[shift_lag][None, :] * jnp.where(same_seq[:, None], shifted, 0.0)
    activated = jax.nn.silu(conv_sum)
    head_in = activated[:, :head_count * MP].reshape(total_rows, head_count, MP)
    state_in = activated[:, head_count * MP:head_count * MP + NS]
    state_out = activated[:, head_count * MP + NS:]
    step_size = jax.nn.softplus(step_raw + bias_step[None, :])
    log_rates = -step_size * jnp.exp(log_rate)[None, :]
    cumulative = jnp.cumsum(log_rates, axis=0).T
    intersection = jnp.dot(state_out, state_in.T, precision=highest)
    log_gap = cumulative[:, :, None] - cumulative[:, None, :]
    decay_mat = jnp.exp(jnp.where(allowed[None, :, :], log_gap, masked_score))
    mixing = intersection[None, :, :] * decay_mat * step_size.T[:, None, :]
    result = jnp.einsum('hts,shp->thp', mixing, head_in, precision=highest) + skip_gain[None, :, None] * head_in
    return result.reshape(total_rows, head_count * MP)

def layer_group(params, hidden_in, cotangent, segment_ids, positions):
    w_query, w_key, w_value, w_mamba_gate, w_mamba_in, w_mamba_bcdt, w_attention_out, w_mamba_out, w_feed_gate, w_feed_up, w_feed_down, gain_mixer, gain_feed, conv_weight, log_decay, step_bias, skip_scale = params
    length = hidden_in.shape[0]
    dev_groups = N_SEQ * N_TENSOR
    heads_dev = MH // dev_groups
    mamba_width = heads_dev * MP
    score_scale = HD ** (-0.5)
    allowed = (segment_ids[:, None] == segment_ids[None, :]) & (positions[None, :] <= positions[:, None])
    cosine, sine_vals = rope_angles(positions, HD)
    core = functools.partial(mamba_core, segment_ids=segment_ids, allowed=allowed)
    normed_one, scale_one, mixer_in = rms_forward(hidden_in, gain_mixer)
    query_all = rotate(matmul(mixer_in, w_query).reshape(length, QH, HD), cosine, sine_vals).astype(jnp.bfloat16).transpose(1, 0, 2)
    key_all = rotate(matmul(mixer_in, w_key).reshape(length, KVH, HD), cosine, sine_vals).astype(jnp.bfloat16).transpose(1, 0, 2)
    value_all = matmul(mixer_in, w_value).reshape(length, KVH, HD).astype(jnp.bfloat16).transpose(1, 0, 2)
    gate_pre = matmul(mixer_in, w_mamba_gate)
    mamba_low = matmul(mixer_in, w_mamba_in).astype(jnp.bfloat16)
    bcdt_low = matmul(mixer_in, w_mamba_bcdt).astype(jnp.bfloat16)

    def device_inputs(group_index):
        x_cols = lax.dynamic_slice_in_dim(mamba_low, group_index * mamba_width, mamba_width, 1)
        mixed_in = jnp.concatenate([x_cols, bcdt_low[:, :2 * NS]], axis=1).astype(jnp.float32)
        step_raw = lax.dynamic_slice_in_dim(bcdt_low, 2 * NS + group_index * heads_dev, heads_dev, 1).astype(jnp.float32)
        conv_taps = jnp.concatenate([lax.dynamic_slice_in_dim(conv_weight, group_index * mamba_width, mamba_width, 1), conv_weight[:, MD:]], axis=1)
        log_rate = lax.dynamic_slice_in_dim(log_decay, group_index * heads_dev, heads_dev, 0)
        bias_step = lax.dynamic_slice_in_dim(step_bias, group_index * heads_dev, heads_dev, 0)
        skip_gain = lax.dynamic_slice_in_dim(skip_scale, group_index * heads_dev, heads_dev, 0)
        return (mixed_in, step_raw, conv_taps, log_rate, bias_step, skip_gain)

    def forward_one(group_index):
        attended, logsum = attend_forward(query_all[group_index], key_all[group_index // N_SEQ], value_all[group_index // N_SEQ], allowed, score_scale)
        ssm_low = core(*device_inputs(group_index)).astype(jnp.bfloat16)
        return (attended, logsum, ssm_low)
    group_ids = jnp.arange(dev_groups, dtype=jnp.int32)
    attended_all, logsum_all, ssm_all = lax.map(forward_one, group_ids)
    attention_cat = attended_all.transpose(1, 0, 2).reshape(length, QCOL)
    ssm_cat = ssm_all.transpose(1, 0, 2).reshape(length, MD)
    silu_gate = jax.nn.silu(gate_pre)
    gated = (ssm_cat.astype(jnp.float32) * silu_gate).astype(jnp.bfloat16)
    middle = hidden_in + (matmul(attention_cat, w_attention_out) + matmul(gated, w_mamba_out))
    normed_two, scale_two, feed_in = rms_forward(middle, gain_feed)
    feed_gate = matmul(feed_in, w_feed_gate)
    feed_up = matmul(feed_in, w_feed_up)
    activated = (jax.nn.silu(feed_gate) * feed_up).astype(jnp.bfloat16)
    output = middle + matmul(activated, w_feed_down)
    cot_low = cotangent.astype(jnp.bfloat16)
    grad_w_feed_down = outer_product(activated, cot_low)
    grad_act = back_product(cot_low, w_feed_down)
    grad_feed_gate_in = (grad_act * feed_up * silu_slope(feed_gate)).astype(jnp.bfloat16)
    grad_feed_up_in = (grad_act * jax.nn.silu(feed_gate)).astype(jnp.bfloat16)
    grad_w_feed_gate = outer_product(feed_in, grad_feed_gate_in)
    grad_w_feed_up = outer_product(feed_in, grad_feed_up_in)
    grad_feed_in = back_product(grad_feed_gate_in, w_feed_gate) + back_product(grad_feed_up_in, w_feed_up)
    grad_middle, grad_gain_feed = rms_backward(grad_feed_in, normed_two, scale_two, gain_feed, cotangent)
    middle_low = grad_middle.astype(jnp.bfloat16)
    grad_w_attention_out = outer_product(attention_cat, middle_low)
    grad_w_mamba_out = outer_product(gated, middle_low)
    grad_gated = back_product(middle_low, w_mamba_out)
    grad_attended = back_product(middle_low, w_attention_out).astype(jnp.bfloat16)
    grad_ssm = (grad_gated * silu_gate).astype(jnp.bfloat16)
    grad_gate_in = (grad_gated * ssm_cat.astype(jnp.float32) * silu_slope(gate_pre)).astype(jnp.bfloat16)
    grad_att_heads = grad_attended.reshape(length, QH, HD).transpose(1, 0, 2)
    grad_ssm_heads = grad_ssm.reshape(length, dev_groups, mamba_width).transpose(1, 0, 2)

    def backward_one(group_index):
        key_in = key_all[group_index // N_SEQ]
        value_in = value_all[group_index // N_SEQ]
        query_in = query_all[group_index]
        grad_query, grad_key, grad_value = attend_backward(query_in, key_in, value_in, allowed, score_scale, attended_all[group_index], logsum_all[group_index], grad_att_heads[group_index])
        query_low = rotate(grad_query[:, None, :], cosine, -sine_vals)[:, 0, :].astype(jnp.bfloat16)
        key_low = rotate(grad_key[:, None, :], cosine, -sine_vals)[:, 0, :].astype(jnp.bfloat16)
        value_low = grad_value.astype(jnp.bfloat16)
        core_out, pullback = jax.vjp(core, *device_inputs(group_index))
        core_grads = pullback(grad_ssm_heads[group_index].astype(jnp.float32))
        return (query_low, key_low, value_low, core_grads[0].astype(jnp.bfloat16), core_grads[1].astype(jnp.bfloat16), core_grads[2], core_grads[3], core_grads[4], core_grads[5])
    dq_all, dk_all, dv_all, dmix_all, dstep_all, dconv_all, drate_all, dbias_all, dskip_all = lax.map(backward_one, group_ids)
    dq_low = dq_all.transpose(1, 0, 2).reshape(length, QCOL)
    dk_low = lax.optimization_barrier(jnp.sum(dk_all.astype(jnp.float32).reshape(KVH, N_SEQ, length, HD), axis=1)).transpose(1, 0, 2).reshape(length, KVCOL).astype(jnp.bfloat16)
    dv_low = lax.optimization_barrier(jnp.sum(dv_all.astype(jnp.float32).reshape(KVH, N_SEQ, length, HD), axis=1)).transpose(1, 0, 2).reshape(length, KVCOL).astype(jnp.bfloat16)
    dx_low = dmix_all[:, :, :mamba_width].transpose(1, 0, 2).reshape(length, MD)
    dstate = lax.optimization_barrier(jnp.sum(dmix_all[:, :, mamba_width:].astype(jnp.float32), axis=0))
    dstep = dstep_all.transpose(1, 0, 2).reshape(length, MH).astype(jnp.float32)
    dbcdt_low = jnp.concatenate([dstate, dstep], axis=1).astype(jnp.bfloat16)
    grad_conv_weight = jnp.concatenate([dconv_all[:, :, :mamba_width].transpose(1, 0, 2).reshape(KCONV, MD), lax.optimization_barrier(jnp.sum(dconv_all[:, :, mamba_width:], axis=0))], axis=1)
    grad_log_decay = drate_all.reshape(MH)
    grad_step_bias = dbias_all.reshape(MH)
    grad_skip_scale = dskip_all.reshape(MH)
    grad_w_query = outer_product(mixer_in, dq_low)
    grad_w_key = outer_product(mixer_in, dk_low)
    grad_w_value = outer_product(mixer_in, dv_low)
    grad_w_mamba_gate = outer_product(mixer_in, grad_gate_in)
    grad_w_mamba_in = outer_product(mixer_in, dx_low)
    grad_w_mamba_bcdt = outer_product(mixer_in, dbcdt_low)
    grad_mixer_in = back_product(dq_low, w_query) + back_product(dk_low, w_key) + back_product(dv_low, w_value) + back_product(grad_gate_in, w_mamba_gate) + back_product(dx_low, w_mamba_in) + back_product(dbcdt_low, w_mamba_bcdt)
    grad_hidden, grad_gain_mixer = rms_backward(grad_mixer_in, normed_one, scale_one, gain_mixer, grad_middle)
    grads = (grad_w_query, grad_w_key, grad_w_value, grad_w_mamba_gate, grad_w_mamba_in, grad_w_mamba_bcdt, grad_w_attention_out, grad_w_mamba_out, grad_w_feed_gate, grad_w_feed_up, grad_w_feed_down, grad_gain_mixer, grad_gain_feed, grad_conv_weight, grad_log_decay, grad_step_bias, grad_skip_scale)
    return (output, grad_hidden, grads)

def reference(hidden_in, cotangent, segment_ids, positions, w_query, w_key, w_value, w_mamba_gate, w_mamba_in, w_mamba_bcdt, w_attention_out, w_mamba_out, w_feed_gate, w_feed_up, w_feed_down, gain_mixer, gain_feed, conv_weight, log_decay, step_bias, skip_scale):
    params = (w_query, w_key, w_value, w_mamba_gate, w_mamba_in, w_mamba_bcdt, w_attention_out, w_mamba_out, w_feed_gate, w_feed_up, w_feed_down, gain_mixer, gain_feed, conv_weight, log_decay, step_bias, skip_scale)
    group_count = hidden_in.shape[0] // GROUP
    stacked = (hidden_in.reshape(group_count, GROUP, D), cotangent.reshape(group_count, GROUP, D), segment_ids.reshape(group_count, GROUP), positions.reshape(group_count, GROUP))
    zero_grads = jax.tree.map(lambda weight_arr: jnp.zeros(weight_arr.shape, jnp.float32), params)

    def scan_group(totals, inputs):
        output, grad_hidden, grads = layer_group(params, inputs[0], inputs[1], inputs[2], inputs[3])
        return (jax.tree.map(lambda left_sum, right_sum: left_sum + right_sum, totals, grads), (output, grad_hidden))
    totals, (output, grad_hidden) = lax.scan(scan_group, zero_grads, stacked)
    return (output.reshape(group_count * GROUP, D), grad_hidden.reshape(group_count * GROUP, D), totals[0], totals[1], totals[2], totals[3], totals[4], totals[5], totals[6], totals[7], totals[8], totals[9], totals[10], totals[11], totals[12], totals[13], totals[14], totals[15], totals[16])
```

```python
import functools
import math

import jax
import jax.numpy as jnp
from jax import lax
from jax.sharding import PartitionSpec as P

D = 1024
HD = 128
MH = 24
MP = 64
NS = 128
KCONV = 4
MD = 1536


epsilon = 1e-05
rope_base = 100000000000.0
masked_score = -1e30
highest = lax.Precision.HIGHEST


def matmul(left_in, right_in):
    return jnp.dot(left_in, right_in, preferred_element_type=jnp.float32)


def outer_product(left_in, right_in):
    return jnp.einsum("tc,td->cd", left_in, right_in, preferred_element_type=jnp.float32)


def back_product(grad_in, weight_in):
    return jnp.einsum("tc,dc->td", grad_in, weight_in, preferred_element_type=jnp.float32)


def gather_rows(pieces, seq_index, seq_count):
    rows = pieces[0].shape[0] // seq_count
    own = jnp.concatenate(
        [lax.dynamic_slice_in_dim(piece, seq_index * rows, rows, 0) for piece in pieces], axis=1
    )
    return lax.all_gather(own, ("dp", "seq"), axis=0, tiled=True)


def gather_columns(weight_in, seq_index, seq_count):
    rows = weight_in.shape[0] // seq_count
    own = lax.dynamic_slice_in_dim(weight_in, seq_index * rows, rows, 0)
    blocks = lax.all_gather(own, ("dp", "seq"), axis=0, tiled=False)
    return blocks.reshape(-1, weight_in.shape[0], weight_in.shape[1])


def matmul_blocks(left_in, blocks):
    product = jnp.einsum("tk,pkn->tpn", left_in, blocks, preferred_element_type=jnp.float32)
    return product.reshape(left_in.shape[0], -1)


def back_blocks(grad_in, blocks):
    parts = grad_in.reshape(grad_in.shape[0], blocks.shape[0], blocks.shape[2])
    return jnp.einsum("tpn,pkn->tk", parts, blocks, preferred_element_type=jnp.float32)


def gather_tokens(parts):
    return lax.all_gather(jnp.concatenate(parts, axis=1), "dp", axis=0, tiled=True)


def rope_angles(token_pos, head_width):
    half_width = head_width // 2
    freq_index = jnp.arange(half_width, dtype=jnp.float32)
    inverse_freq = jnp.exp(freq_index * (-2.0 * math.log(rope_base) / head_width))
    angles = token_pos.astype(jnp.float32)[:, None] * inverse_freq[None, :]
    return (jnp.cos(angles), jnp.sin(angles))


def rotate(values, cosine, sine_vals):
    half_width = values.shape[-1] // 2
    first_half = values[..., :half_width]
    second_half = values[..., half_width:]
    cos_rows = cosine[:, None, :]
    sin_rows = sine_vals[:, None, :]
    return jnp.concatenate(
        [
            first_half * cos_rows - second_half * sin_rows,
            second_half * cos_rows + first_half * sin_rows,
        ],
        axis=-1,
    )


def rms_forward(values, gain_vec):
    scale_rows = lax.rsqrt(jnp.mean(values * values, axis=1, keepdims=True) + epsilon)
    normed = values * scale_rows
    return (
        normed,
        scale_rows,
        (normed * gain_vec.astype(jnp.float32)[None, :]).astype(jnp.bfloat16),
    )


def rms_backward(grad_out, normed, scale_rows, gain_vec, upstream):
    grad_gain = jnp.sum(grad_out * normed, axis=0)
    grad_normed = grad_out * gain_vec.astype(jnp.float32)[None, :]
    grad_in = upstream + scale_rows * (
        grad_normed - normed * jnp.mean(grad_normed * normed, axis=1, keepdims=True)
    )
    return (grad_in, grad_gain)


def silu_slope(pre_act):
    sigmoid_gate = jax.nn.sigmoid(pre_act)
    return sigmoid_gate * (1.0 + pre_act * (1.0 - sigmoid_gate))


def attend_forward(query_in, key_in, value_in, allowed, score_scale):
    total_rows = query_in.shape[0]
    block_rows = min(total_rows, 512)
    block_count = total_rows // block_rows

    def one_block(block_index):
        scores = (
            jnp.einsum("qd,kd->qk", query_in, key_in, preferred_element_type=jnp.float32)
            * score_scale
        )
        scores = jnp.where(allowed, scores, masked_score)
        row_peak = jnp.max(scores, axis=1, keepdims=True)
        logsum = row_peak + jnp.log(jnp.sum(jnp.exp(scores - row_peak), axis=1, keepdims=True))
        softmax_low = jnp.exp(scores - logsum).astype(jnp.bfloat16)
        result = jnp.dot(softmax_low, value_in, preferred_element_type=jnp.float32).astype(
            jnp.bfloat16
        )
        return (result, logsum[:, 0])

    result, logsum = lax.map(one_block, jnp.arange(block_count, dtype=jnp.int32))
    return (result.reshape(total_rows, value_in.shape[1]), logsum.reshape(total_rows))


def attend_backward(query_in, key_in, value_in, allowed, score_scale, result, logsum, grad_result):
    total_rows, head_width = query_in.shape
    block_rows = min(total_rows, 512)
    block_count = total_rows // block_rows
    row_delta = jnp.sum(grad_result.astype(jnp.float32) * result.astype(jnp.float32), axis=1)

    def one_block(totals, block_index):
        grad_key, grad_value = totals
        scores = (
            jnp.einsum("qd,kd->qk", query_in, key_in, preferred_element_type=jnp.float32)
            * score_scale
        )
        scores = jnp.where(allowed, scores, masked_score)
        softmax_f = jnp.exp(scores - logsum[:, None])
        grad_value = grad_value + jnp.einsum(
            "qk,qd->kd",
            softmax_f.astype(jnp.bfloat16),
            grad_result,
            preferred_element_type=jnp.float32,
        )
        grad_probs = jnp.einsum(
            "qd,kd->qk", grad_result, value_in, preferred_element_type=jnp.float32
        )
        grad_scores = (softmax_f * (grad_probs - row_delta[:, None])).astype(jnp.bfloat16)
        grad_query = jnp.dot(grad_scores, key_in, preferred_element_type=jnp.float32) * score_scale
        grad_key = (
            grad_key
            + jnp.einsum("qk,qd->kd", grad_scores, query_in, preferred_element_type=jnp.float32)
            * score_scale
        )
        return ((grad_key, grad_value), grad_query)

    zero_rows = jnp.zeros((total_rows, head_width), jnp.float32)
    (grad_key, grad_value), grad_query = lax.scan(
        one_block, (zero_rows, zero_rows), jnp.arange(block_count, dtype=jnp.int32)
    )
    return (grad_query.reshape(total_rows, head_width), grad_key, grad_value)


def mamba_core(mixed_in, step_raw, conv_taps, log_rate, bias_step, skip_gain, segment_ids, allowed):
    total_rows, col_width = mixed_in.shape
    head_count = step_raw.shape[1]
    conv_sum = conv_taps[0][None, :] * mixed_in
    for shift_lag in range(1, conv_taps.shape[0]):
        shifted = jnp.concatenate(
            [jnp.zeros((shift_lag, col_width), mixed_in.dtype), mixed_in[:-shift_lag]], axis=0
        )
        same_seq = jnp.concatenate(
            [
                jnp.zeros((shift_lag,), dtype=bool),
                segment_ids[shift_lag:] == segment_ids[:-shift_lag],
            ],
            axis=0,
        )
        conv_sum = conv_sum + conv_taps[shift_lag][None, :] * jnp.where(
            same_seq[:, None], shifted, 0.0
        )
    activated = jax.nn.silu(conv_sum)
    head_in = activated[:, : head_count * MP].reshape(total_rows, head_count, MP)
    state_in = activated[:, head_count * MP : head_count * MP + NS]
    state_out = activated[:, head_count * MP + NS :]
    step_size = jax.nn.softplus(step_raw + bias_step[None, :])
    log_rates = -step_size * jnp.exp(log_rate)[None, :]
    cumulative = jnp.cumsum(log_rates, axis=0).T
    intersection = jnp.dot(state_out, state_in.T, precision=highest)
    log_gap = cumulative[:, :, None] - cumulative[:, None, :]
    decay_mat = jnp.exp(jnp.where(allowed[None, :, :], log_gap, masked_score))
    mixing = intersection[None, :, :] * decay_mat * step_size.T[:, None, :]
    result = (
        jnp.einsum("hts,shp->thp", mixing, head_in, precision=highest)
        + skip_gain[None, :, None] * head_in
    )
    return result.reshape(total_rows, head_count * MP)


def body(
    hidden_in,
    cotangent,
    segment_ids,
    positions,
    w_query,
    w_key,
    w_value,
    w_mamba_gate,
    w_mamba_in,
    w_mamba_bcdt,
    w_attention_out,
    w_mamba_out,
    w_feed_gate,
    w_feed_up,
    w_feed_down,
    gain_mixer,
    gain_feed,
    conv_weight,
    log_decay,
    step_bias,
    skip_scale,
):
    seq_count = lax.axis_size("seq")
    tensor_count = lax.axis_size("tensor")
    seq_index = lax.axis_index("seq")
    tensor_index = lax.axis_index("tensor")
    local_rows = hidden_in.shape[0]
    heads_dev = MH // (seq_count * tensor_count)
    mamba_width = heads_dev * MP
    device_group = tensor_index * seq_count + seq_index
    score_scale = HD ** (-0.5)
    dp_count = lax.axis_size("dp")
    entry_full = gather_rows(
        [
            w_query,
            w_key,
            w_value,
            w_mamba_gate,
            w_mamba_in,
            w_mamba_bcdt,
            gain_mixer[:, None],
            gain_feed[:, None],
        ],
        seq_index,
        seq_count,
    )
    out_blocks = gather_columns(
        jnp.concatenate([w_attention_out, w_mamba_out], axis=0), seq_index, seq_count
    )
    feed_full = gather_rows([w_feed_gate, w_feed_up], seq_index, seq_count)
    down_blocks = gather_columns(w_feed_down, seq_index, seq_count)
    query_end = w_query.shape[1]
    key_end = query_end + w_key.shape[1]
    value_end = key_end + w_value.shape[1]
    gate_end = value_end + w_mamba_gate.shape[1]
    input_end = gate_end + w_mamba_in.shape[1]
    state_end = input_end + w_mamba_bcdt.shape[1]
    attention_width = w_attention_out.shape[0]
    feed_width = w_feed_gate.shape[1]
    full_gain_mixer = entry_full[:, state_end]
    full_gain_feed = entry_full[:, state_end + 1]
    allowed = (segment_ids[:, None] == segment_ids[None, :]) & (
        positions[None, :] <= positions[:, None]
    )
    cosine, sine_vals = rope_angles(positions, HD)
    local_cos = lax.dynamic_slice_in_dim(cosine, seq_index * local_rows, local_rows, 0)
    local_sin = lax.dynamic_slice_in_dim(sine_vals, seq_index * local_rows, local_rows, 0)
    core = functools.partial(mamba_core, segment_ids=segment_ids, allowed=allowed)
    normed_one, scale_one, mixer_in = rms_forward(hidden_in, full_gain_mixer)
    entry_pre = matmul(mixer_in, entry_full)
    query_rot = rotate(
        entry_pre[:, :query_end].reshape(local_rows, seq_count, HD), local_cos, local_sin
    )
    key_rot = rotate(
        entry_pre[:, query_end:key_end].reshape(local_rows, 1, HD), local_cos, local_sin
    )
    value_pre = entry_pre[:, key_end:value_end].reshape(local_rows, 1, HD)
    gate_pre = entry_pre[:, value_end:gate_end]
    mamba_pre = entry_pre[:, gate_end:input_end].reshape(local_rows, seq_count, mamba_width)
    bcdt_pre = entry_pre[:, input_end:state_end]
    state_pre = jnp.broadcast_to(bcdt_pre[:, None, : 2 * NS], (local_rows, seq_count, 2 * NS))
    step_pre = lax.dynamic_slice_in_dim(
        bcdt_pre, 2 * NS + tensor_index * seq_count * heads_dev, seq_count * heads_dev, 1
    )
    step_pre = step_pre.reshape(local_rows, seq_count, heads_dev)
    spread_shape = (local_rows, seq_count, HD)
    packed = jnp.concatenate(
        [
            query_rot,
            jnp.broadcast_to(key_rot, spread_shape),
            jnp.broadcast_to(value_pre, spread_shape),
            mamba_pre,
            state_pre,
            step_pre,
        ],
        axis=2,
    ).astype(jnp.bfloat16)
    arrived = lax.all_to_all(packed, "seq", split_axis=1, concat_axis=0, tiled=True)[:, 0, :]
    head_query = arrived[:, :HD]
    head_key = arrived[:, HD : 2 * HD]
    head_value = arrived[:, 2 * HD : 3 * HD]
    mixed_low = arrived[:, 3 * HD : 3 * HD + mamba_width + 2 * NS]
    step_low = arrived[:, 3 * HD + mamba_width + 2 * NS :]
    conv_taps = jnp.concatenate(
        [
            lax.dynamic_slice_in_dim(conv_weight, device_group * mamba_width, mamba_width, 1),
            conv_weight[:, MD:],
        ],
        axis=1,
    )
    log_rate = lax.dynamic_slice_in_dim(log_decay, device_group * heads_dev, heads_dev, 0)
    bias_step = lax.dynamic_slice_in_dim(step_bias, device_group * heads_dev, heads_dev, 0)
    skip_gain = lax.dynamic_slice_in_dim(skip_scale, device_group * heads_dev, heads_dev, 0)
    attended, logsum = attend_forward(head_query, head_key, head_value, allowed, score_scale)
    ssm_f32, pullback = jax.vjp(
        core,
        mixed_low.astype(jnp.float32),
        step_low.astype(jnp.float32),
        conv_taps,
        log_rate,
        bias_step,
        skip_gain,
    )
    ssm_low = ssm_f32.astype(jnp.bfloat16)
    returned = lax.all_to_all(
        jnp.concatenate([attended, ssm_low], axis=1)[:, None, :],
        "seq",
        split_axis=0,
        concat_axis=1,
        tiled=True,
    )
    attention_cat = returned[:, :, :HD].reshape(local_rows, seq_count * HD)
    ssm_cat = returned[:, :, HD:].reshape(local_rows, seq_count * mamba_width)
    silu_gate = jax.nn.silu(gate_pre)
    gated = (ssm_cat.astype(jnp.float32) * silu_gate).astype(jnp.bfloat16)
    mixer_part = matmul_blocks(jnp.concatenate([attention_cat, gated], axis=1), out_blocks)
    middle = hidden_in + lax.psum(mixer_part, "tensor")
    normed_two, scale_two, feed_in = rms_forward(middle, full_gain_feed)
    feed_pre = matmul(feed_in, feed_full)
    feed_gate = feed_pre[:, :feed_width]
    feed_up = feed_pre[:, feed_width:]
    activated = (jax.nn.silu(feed_gate) * feed_up).astype(jnp.bfloat16)
    output = middle + lax.psum(
        matmul_blocks(activated, down_blocks).astype(jnp.bfloat16), "tensor"
    ).astype(jnp.float32)
    cot_low = cotangent.astype(jnp.bfloat16)
    grad_act = back_blocks(cot_low, down_blocks)
    grad_feed_gate_in = (grad_act * feed_up * silu_slope(feed_gate)).astype(jnp.bfloat16)
    grad_feed_up_in = (grad_act * jax.nn.silu(feed_gate)).astype(jnp.bfloat16)
    feed_part = back_product(
        jnp.concatenate([grad_feed_gate_in, grad_feed_up_in], axis=1), feed_full
    )
    feed_tokens = gather_tokens([grad_feed_gate_in, grad_feed_up_in, activated])
    grad_feed_in = lax.psum(feed_part, "tensor")
    grad_middle, grad_gain_feed = rms_backward(
        grad_feed_in, normed_two, scale_two, full_gain_feed, cotangent
    )
    middle_low = grad_middle.astype(jnp.bfloat16)
    grad_out = back_blocks(middle_low, out_blocks)
    grad_gated = grad_out[:, attention_width:]
    grad_attended = grad_out[:, :attention_width].astype(jnp.bfloat16)
    grad_ssm = (grad_gated * silu_gate).astype(jnp.bfloat16)
    grad_gate_in = (grad_gated * ssm_cat.astype(jnp.float32) * silu_slope(gate_pre)).astype(
        jnp.bfloat16
    )
    outgoing = jnp.concatenate(
        [
            grad_attended.reshape(local_rows, seq_count, HD),
            grad_ssm.reshape(local_rows, seq_count, mamba_width),
        ],
        axis=2,
    )
    head_grads = lax.all_to_all(outgoing, "seq", split_axis=1, concat_axis=0, tiled=True)[:, 0, :]
    grad_query, grad_key, grad_value = attend_backward(
        head_query, head_key, head_value, allowed, score_scale, attended, logsum, head_grads[:, :HD]
    )
    query_low = rotate(grad_query[:, None, :], cosine, -sine_vals)[:, 0, :].astype(jnp.bfloat16)
    key_low = rotate(grad_key[:, None, :], cosine, -sine_vals)[:, 0, :].astype(jnp.bfloat16)
    value_low = grad_value.astype(jnp.bfloat16)
    core_grads = pullback(head_grads[:, HD:].astype(jnp.float32))
    back_pack = jnp.concatenate(
        [
            query_low,
            key_low,
            value_low,
            core_grads[0].astype(jnp.bfloat16),
            core_grads[1].astype(jnp.bfloat16),
        ],
        axis=1,
    )
    token_grads = lax.all_to_all(
        back_pack[:, None, :], "seq", split_axis=0, concat_axis=1, tiled=True
    )
    dq_low = token_grads[:, :, :HD].reshape(local_rows, seq_count * HD)
    dk_low = jnp.sum(token_grads[:, :, HD : 2 * HD].astype(jnp.float32), axis=1).astype(
        jnp.bfloat16
    )
    dv_low = jnp.sum(token_grads[:, :, 2 * HD : 3 * HD].astype(jnp.float32), axis=1).astype(
        jnp.bfloat16
    )
    dx_low = token_grads[:, :, 3 * HD : 3 * HD + mamba_width].reshape(
        local_rows, seq_count * mamba_width
    )
    state_part = jnp.sum(
        token_grads[:, :, 3 * HD + mamba_width : 3 * HD + mamba_width + 2 * NS].astype(jnp.float32),
        axis=1,
    )
    step_own = (
        token_grads[:, :, 3 * HD + mamba_width + 2 * NS :]
        .reshape(local_rows, seq_count * heads_dev)
        .astype(jnp.float32)
    )
    step_part = lax.dynamic_update_slice_in_dim(
        jnp.zeros((local_rows, MH), jnp.float32), step_own, tensor_index * seq_count * heads_dev, 1
    )
    bcdt_part = jnp.concatenate([state_part, step_part], axis=1)
    input_part = back_product(
        jnp.concatenate([dq_low, dk_low, dv_low, grad_gate_in, dx_low], axis=1),
        entry_full[:, :input_end],
    )
    input_sum, bcdt_sum = lax.psum((input_part, bcdt_part), "tensor")
    dbcdt_low = bcdt_sum.astype(jnp.bfloat16)
    grad_mixer_in = input_sum + back_product(dbcdt_low, entry_full[:, input_end:state_end])
    grad_hidden, grad_gain_mixer = rms_backward(
        grad_mixer_in, normed_one, scale_one, full_gain_mixer, grad_middle
    )
    conv_size = KCONV * mamba_width
    state_size = KCONV * 2 * NS
    small_own = jnp.concatenate(
        [
            core_grads[2][:, :mamba_width].reshape(conv_size),
            core_grads[2][:, mamba_width:].reshape(state_size),
            core_grads[3],
            core_grads[4],
            core_grads[5],
            grad_gain_mixer,
            grad_gain_feed,
        ]
    )
    small_size = -(-small_own.shape[0] // 1024) * 1024
    small_own = jnp.pad(small_own, (0, small_size - small_own.shape[0])).reshape(-1, 128)
    small_all = lax.all_gather(small_own, ("dp", "seq", "tensor"), axis=0, tiled=True)
    small_all = small_all.reshape(dp_count, seq_count, tensor_count, small_size)
    head_start = conv_size + state_size
    gain_start = head_start + 3 * heads_dev
    small_sum = jnp.sum(small_all[..., :gain_start], axis=0)
    conv_x = small_sum[..., :conv_size].reshape(seq_count, tensor_count, KCONV, mamba_width)
    conv_x = conv_x.transpose(2, 1, 0, 3).reshape(KCONV, MD)
    conv_state = jnp.sum(small_sum[..., conv_size:head_start], axis=(0, 1))
    grad_conv_weight = jnp.concatenate([conv_x, conv_state.reshape(KCONV, 2 * NS)], axis=1)
    head_sum = small_sum[..., head_start:].reshape(seq_count, tensor_count, 3, heads_dev)
    head_sum = head_sum.transpose(2, 1, 0, 3).reshape(3, MH)
    grad_log_decay, grad_step_bias, grad_skip_scale = head_sum[0], head_sum[1], head_sum[2]
    owner_rows = D // dp_count
    owner_start = lax.axis_index("dp") * owner_rows
    gain_all = small_all[:, :, 0, gain_start : gain_start + 2 * D].reshape(dp_count * seq_count, 2, D)
    owned_gain = jnp.sum(
        lax.dynamic_slice_in_dim(gain_all, owner_start, owner_rows, 2), axis=0
    )
    owned_gain_mixer, owned_gain_feed = owned_gain[0], owned_gain[1]
    column_shape = (local_rows, dp_count, owner_rows)
    column_tokens = lax.all_to_all(
        jnp.concatenate(
            [
                mixer_in.reshape(column_shape),
                feed_in.reshape(column_shape),
                cot_low.reshape(column_shape),
                middle_low.reshape(column_shape),
            ],
            axis=2,
        ),
        "dp",
        split_axis=1,
        concat_axis=0,
        tiled=True,
    )[:, 0, :]
    mixer_cols = column_tokens[:, :owner_rows]
    feed_cols = column_tokens[:, owner_rows : 2 * owner_rows]
    cot_cols = column_tokens[:, 2 * owner_rows : 3 * owner_rows]
    middle_cols = column_tokens[:, 3 * owner_rows :]
    middle_tokens = gather_tokens([attention_cat, gated, grad_gate_in])
    gated_end = attention_width + gated.shape[1]
    input_tokens = gather_tokens([dq_low, dk_low, dv_low, dx_low, dbcdt_low])
    low = jnp.bfloat16
    grad_feed = outer_product(feed_cols, feed_tokens[:, : 2 * feed_width]).astype(low)
    grad_down = outer_product(feed_tokens[:, 2 * feed_width :], cot_cols).astype(low)
    grad_out_rows = outer_product(middle_tokens[:, :gated_end], middle_cols).astype(low)
    grad_gate_cols = outer_product(mixer_cols, middle_tokens[:, gated_end:]).astype(low)
    grad_entry = outer_product(mixer_cols, input_tokens).astype(low)
    grad_feed, grad_down, grad_out_rows, grad_gate_cols, grad_entry = (
        total.astype(jnp.float32)
        for total in lax.psum(
            (grad_feed, grad_down, grad_out_rows, grad_gate_cols, grad_entry), "seq"
        )
    )
    dx_end = value_end + w_mamba_in.shape[1]
    owned = (
        grad_entry[:, :query_end],
        grad_entry[:, query_end:key_end],
        grad_entry[:, key_end:value_end],
        grad_gate_cols,
        grad_entry[:, value_end:dx_end],
        grad_entry[:, dx_end:],
        grad_out_rows[:attention_width],
        grad_out_rows[attention_width:],
        grad_feed[:, :feed_width],
        grad_feed[:, feed_width:],
        grad_down,
    )
    return (
        output,
        grad_hidden,
        owned[0],
        owned[1],
        owned[2],
        owned[3],
        owned[4],
        owned[5],
        owned[6],
        owned[7],
        owned[8],
        owned[9],
        owned[10],
        owned_gain_mixer,
        owned_gain_feed,
        grad_conv_weight,
        grad_log_decay,
        grad_step_bias,
        grad_skip_scale,
    )


def solution(mesh):
    return jax.shard_map(
        body,
        mesh=mesh,
        in_specs=(
            P(("dp", "seq"), None),
            P(("dp", "seq"), None),
            P("dp"),
            P("dp"),
            P("dp", "tensor"),
            P("dp", "tensor"),
            P("dp", "tensor"),
            P("dp", "tensor"),
            P("dp", "tensor"),
            P("dp", None),
            P("tensor", "dp"),
            P("tensor", "dp"),
            P("dp", "tensor"),
            P("dp", "tensor"),
            P("tensor", "dp"),
            P("dp"),
            P("dp"),
            P(),
            P(),
            P(),
            P(),
        ),
        out_specs=(
            P(("dp", "seq"), None),
            P(("dp", "seq"), None),
            P("dp", "tensor"),
            P("dp", "tensor"),
            P("dp", "tensor"),
            P("dp", "tensor"),
            P("dp", "tensor"),
            P("dp", None),
            P("tensor", "dp"),
            P("tensor", "dp"),
            P("dp", "tensor"),
            P("dp", "tensor"),
            P("tensor", "dp"),
            P("dp"),
            P("dp"),
            P(),
            P(),
            P(),
            P(),
        ),
        check_vma=False,
    )
```
